32 devices in a mesh: lat: 8 (over y, x, core), lev: 4 (over z).
Axes of the slice: x: 2, y: 2, z: 4, core: 2. Of those that a mesh axis runs over, the one named last changes fastest.
Arguments:
- grid_adjoint: float32 [2, 96, 640, 1280], P(None, 'lev', 'lat'), may hold values from -6 to 6
- trajectory: bfloat16 [2, 96, 640, 1280], P(None, 'lev', 'lat'), may hold values from -5 to 5
- pair_order: int32 [320], replicated, may hold values from 0 to 319, each once
- legendre: bfloat16 [320, 640, 641], P('lat'), may hold values from -0.25 to 0.25
- modes: bfloat16 [96, 96], replicated, may hold values from -0.625 to 0.625
- rates: float32 [96], replicated, may hold values from 0.5 to 50
Outputs:
- grid_out: float32 [2, 96, 640, 1280], P(None, 'lev', 'lat')
The draws below stay inside these ranges and needn't reach their ends.
Inputs may be any that keep to these rules, and one draw needn't show every extreme that they name: `pair_order`: A permutation: entry s names the pair k and 639 - k whose basis values are row s of legendre.
All inputs are finite; a program needn't handle non-finite values.
Results may differ from the reference program's by a relative error of at most 0.0068.
Values may be sent and summed in bfloat16 or wider, within the bound.
A program may use at most 192 MiB of HBM per device.

```python
import math
import jax
import jax.numpy as jnp
from jax import lax

NLON = 1280
NLAT = 640
LEV = 96
NTRUNC = 640
PAIRS = 320


def level_of(rng, dims, cuts, least, largest):
    factor_of = 1.0
    for axis_at, shards_of in cuts:
        heights = jax.random.uniform(jax.random.fold_in(jax.random.fold_in(rng, 6), axis_at), (shards_of,), jnp.float32, least / len(cuts), largest / len(cuts))
        factor_of = factor_of * jnp.repeat(jnp.exp(heights), dims[axis_at] // shards_of).reshape((-1,) + (1,) * (len(dims) - 1 - axis_at))
    return factor_of


def bell_draw(rng, dims, width, reach, shards=(), kind=jnp.bfloat16):
    level = level_of(rng, dims, shards, -0.22, 0.18) if shards else 1.0
    drawn = jax.random.normal(rng, dims, jnp.float32) * width * level
    return jnp.minimum(jnp.maximum(drawn, -reach), reach).astype(kind)


def setup_inputs(seed: int = 0) -> dict:
    key_list = jax.random.split(jax.random.key(seed), 7)
    return {
        "grid_adjoint": bell_draw(key_list[0], (2, LEV, NLAT, NLON), 1.0, 6.0, ((1, 4), (2, 8)), jnp.float32),
        "trajectory": bell_draw(key_list[1], (2, LEV, NLAT, NLON), 1.0, 5.0, ((1, 4), (2, 8))),
        "pair_order": jax.random.permutation(key_list[2], PAIRS).astype(jnp.int32),
        "legendre": bell_draw(key_list[3], (PAIRS, NLAT, NTRUNC + 1), NLAT ** -0.5, 0.25, ((0, 8),)),
        "modes": bell_draw(key_list[4], (LEV, LEV), LEV ** -0.5, 0.625),
        "rates": jnp.clip(jnp.exp(jax.random.uniform(key_list[5], (LEV,), jnp.float32, math.log(0.5), math.log(50.0))), 0.5, 50.0),
    }


def tables(length, number):
    row = lax.broadcasted_iota(jnp.int32, (length, 2 * number), 0)
    col = lax.broadcasted_iota(jnp.int32, (length, 2 * number), 1)
    wavenum = col % number
    phases = (2.0 * math.pi / length) * ((row * wavenum) % length).astype(jnp.float32)
    forward = (jnp.where(col < number, jnp.cos(phases), -jnp.sin(phases)) / length).astype(jnp.bfloat16)
    inrow = lax.broadcasted_iota(jnp.int32, (2 * number, length), 0)
    position = lax.broadcasted_iota(jnp.int32, (2 * number, length), 1)
    inwave = inrow % number
    inphase = (2.0 * math.pi / length) * ((position * inwave) % length).astype(jnp.float32)
    weights = jnp.where(inwave == 0, 1.0, 2.0).astype(jnp.float32)
    inverse = jnp.where(inrow < number, weights * jnp.cos(inphase), -weights * jnp.sin(inphase)).astype(jnp.bfloat16)
    return forward, inverse


def degrees(waves_a, truncation):
    column = lax.broadcasted_iota(jnp.int32, (waves_a.shape[0], truncation + 1), 1)
    lower_part = column < (truncation - waves_a)[:, None]
    degree = jnp.where(lower_part, waves_a[:, None] + column, column - 1)
    degree_ratio = (degree * (degree + 1)).astype(jnp.float32) / float(truncation * (truncation + 1))
    return lower_part, degree_ratio


def reference(grid_adjoint, trajectory, pair_order, legendre, modes, rates):
    highest = lax.Precision.HIGHEST
    primary = trajectory[0].astype(jnp.float32)
    coupling = trajectory[1].astype(jnp.float32)
    coupled = jnp.stack([primary * grid_adjoint[0] + coupling * grid_adjoint[1],
                         coupling * grid_adjoint[0] + primary * grid_adjoint[1]]).astype(jnp.bfloat16)
    forward, inverse = tables(NLON, NTRUNC)
    fourier = jnp.dot(coupled.reshape(-1, NLON), forward,
                      preferred_element_type=jnp.float32).astype(jnp.bfloat16).reshape(2, LEV, NLAT, 2, NTRUNC)
    column_order = jnp.stack([pair_order, NTRUNC - 1 - pair_order], axis=1).astype(jnp.int32)
    lower_part, degree_ratio = degrees(pair_order.astype(jnp.int32), NTRUNC)

    def analyse(entry):
        basis, columns, lower_mask = entry
        picked = jnp.take(fourier, columns, axis=4)
        products = jnp.einsum("lj,fvlch->fvchj", basis.astype(jnp.float32), picked.astype(jnp.float32),
                              precision=highest)
        return jnp.where(lower_mask, products[:, :, :, 0], products[:, :, :, 1])

    spectral = lax.map(analyse, (legendre, column_order, lower_part))
    damped = spectral[:, 0] / (1.0 + 4.0 * degree_ratio * degree_ratio)[:, None, None, :]
    rounded = spectral[:, 1].astype(jnp.bfloat16)
    projected = jnp.einsum("km,skcj->smcj", modes.astype(jnp.float32), rounded.astype(jnp.float32))
    factor = 1.0 / (1.0 + rates[None, :, None] * degree_ratio[:, None, :])
    weighted = (projected * factor[:, :, None, :]).astype(jnp.bfloat16)
    solved = jnp.einsum("vm,smcj->svcj", modes.astype(jnp.float32), weighted.astype(jnp.float32))
    updated = jnp.stack([damped, solved], axis=1).astype(jnp.bfloat16)

    def synthesise(entry):
        basis, values, lower_mask = entry
        values = values.astype(jnp.float32)
        halves = jnp.stack([jnp.where(lower_mask, values, 0.0), jnp.where(lower_mask, 0.0, values)], axis=-2)
        return jnp.einsum("lj,fvchj->fvlch", basis.astype(jnp.float32), halves,
                          precision=highest).astype(jnp.bfloat16)

    pieces = lax.map(synthesise, (legendre, updated, lower_part))
    shifted_axes = jnp.transpose(pieces, (1, 2, 3, 4, 0, 5)).reshape(2, LEV, NLAT, 2, NTRUNC)
    flattened = column_order.reshape(-1)
    inverse_order = jnp.zeros((NTRUNC,), jnp.int32).at[flattened].set(jnp.arange(NTRUNC, dtype=jnp.int32))
    returned = jnp.take(shifted_axes, inverse_order, axis=4)
    grid_out = jnp.dot(returned.reshape(-1, 2 * NTRUNC), inverse, preferred_element_type=jnp.float32)
    return grid_out.reshape(2, LEV, NLAT, NLON)
```

```python
import functools
import math

import jax
import jax.numpy as jnp
from jax import lax
from jax.experimental import pallas as pl
from jax.experimental.pallas import tpu as pltpu
from jax.sharding import PartitionSpec as P


def circle(waves, length):
    step = math.gcd(length, 32)
    coarse = jnp.arange(length // step, dtype=jnp.int32) * step
    fine = jnp.arange(step, dtype=jnp.int32)

    def angles(position):
        turns = (waves[:, None] * position[None, :]) % length
        phases = 2.0 * math.pi / length * turns.astype(jnp.float32)
        return jnp.cos(phases), jnp.sin(phases)

    cos_a, sin_a = angles(coarse)
    cos_b, sin_b = angles(fine)
    return lax.optimization_barrier((cos_a, sin_a, cos_b, sin_b))


def expand(parts, imaginary, length):
    cos_a, sin_a, cos_b, sin_b = parts
    count = cos_a.shape[0]
    wide = lambda t: jnp.repeat(t, length // t.shape[1], axis=1)
    tall = lambda t: jnp.tile(t, (1, length // t.shape[1]))
    ca, sa, cb, sb = wide(cos_a), wide(sin_a), tall(cos_b), tall(sin_b)
    return jnp.where(imaginary[:, None], -(sa * cb + ca * sb), ca * cb - sa * sb)


def ratio_of(wave_a, column, truncation):
    lower = column < truncation - wave_a
    degree = jnp.where(lower, wave_a + column, column - 1)
    ratio = (degree * (degree + 1)).astype(jnp.float32) / float(truncation * (truncation + 1))
    return lower, ratio


def analysed(x, leg, wave_a, truncation, damp):
    rows = x.shape[0] // 2
    product = lax.dot_general(
        x, leg, (((1,), (1,)), ((), ())), preferred_element_type=jnp.float32
    )
    column = lax.broadcasted_iota(jnp.int32, (rows, product.shape[1]), 1)
    lower, ratio = ratio_of(wave_a, column, truncation)
    chosen = jnp.where(lower, product[:rows], product[rows:])
    if damp:
        chosen = chosen / (1.0 + 4.0 * ratio * ratio)
    return chosen.astype(jnp.bfloat16)


def synthesised(values, leg, wave_a, truncation):
    column = lax.broadcasted_iota(jnp.int32, values.shape, 1)
    lower = column < truncation - wave_a
    zero = jnp.zeros_like(values)
    halves = jnp.concatenate([jnp.where(lower, values, zero), jnp.where(lower, zero, values)], axis=0)
    return jnp.dot(halves, leg, preferred_element_type=jnp.float32).astype(jnp.bfloat16)


def slot_kernel(stages, truncation, waves_ref, in_ref, leg_ref, out_ref):
    group = leg_ref.shape[0]
    for i in range(group):
        wave_a = waves_ref[pl.program_id(0) * group + i]
        value, leg = in_ref[i], leg_ref[i]
        if "analyse" in stages:
            value = analysed(value, leg, wave_a, truncation, "damp" in stages)
        if "synthesise" in stages:
            value = synthesised(value, leg, wave_a, truncation)
        out_ref[i] = value


def slot_call(stages, truncation, waves, values, legendre, rows, width):
    slots, columns, lat_count = legendre.shape
    inner = values.shape[1:]
    group = max(g for g in (1, 2, 4) if slots % g == 0)
    return pl.pallas_call(
        functools.partial(slot_kernel, stages, truncation),
        grid_spec=pltpu.PrefetchScalarGridSpec(
            num_scalar_prefetch=1,
            grid=(slots // group,),
            in_specs=[
                pl.BlockSpec((group,) + inner, lambda s, w: (s, 0, 0)),
                pl.BlockSpec((group, columns, lat_count), lambda s, w: (s, 0, 0)),
            ],
            out_specs=pl.BlockSpec((group, rows, width), lambda s, w: (s, 0, 0)),
        ),
        out_shape=jax.ShapeDtypeStruct((slots, rows, width), jnp.bfloat16),
        cost_estimate=pl.CostEstimate(
            flops=2 * slots * max(rows, inner[0]) * lat_count * columns,
            bytes_accessed=2 * slots * (lat_count * columns + inner[0] * inner[1] + rows * width),
            transcendentals=0,
        ),
    )(waves, values, legendre)


def swap(x, axis):
    n = lax.axis_size(axis)
    me = lax.axis_index(axis)
    size = x.shape[0] // n
    pieces = []
    for k in range(n):
        piece = lax.dynamic_slice_in_dim(x, (me + k) % n * size, size, 0)
        if k:
            piece = lax.ppermute(piece, axis, [(i, (i + k) % n) for i in range(n)])
        pieces.append(piece)
    out = jnp.zeros_like(x)
    for k, piece in enumerate(pieces):
        out = lax.dynamic_update_slice_in_dim(out, piece, (me - k + n) % n * size, 0)
    return out


def per_device(grid_adjoint, trajectory, pair_order, legendre, modes, rates):
    fields, levels, lat_rows, length = grid_adjoint.shape
    truncation = length // 2
    slots, lat_count, columns = legendre.shape
    legendre = jnp.transpose(legendre, (0, 2, 1))
    bands = lax.axis_size("lat")
    layers = lax.axis_size("lev")
    points = levels * lat_rows
    pair_order = pair_order.astype(jnp.int32)

    both = jnp.stack([pair_order, truncation - 1 - pair_order], axis=1)
    waves = jnp.repeat(both.reshape(-1), 2)
    imaginary = jnp.arange(4 * pair_order.shape[0]) % 2 == 1
    parts = circle(waves, length)
    forward = (expand(parts, imaginary, length) / length).astype(jnp.bfloat16)
    weight = jnp.where(waves == 0, 1.0, 2.0).astype(jnp.float32)

    local_waves = lax.dynamic_slice_in_dim(pair_order, lax.axis_index("lat") * slots, slots)

    def to_fourier(f):
        own = trajectory[0].astype(jnp.float32) * grid_adjoint[f]
        other = trajectory[1].astype(jnp.float32) * grid_adjoint[1 - f]
        coupled = (own + other).astype(jnp.bfloat16).reshape(points, length)
        fourier = lax.dot_general(
            forward, coupled, (((1,), (1,)), ((), ())), preferred_element_type=jnp.float32
        ).astype(jnp.bfloat16)
        return fourier.reshape(bands, slots * 4, points)

    def exchange(sent):
        return lax.all_to_all(sent, "lat", split_axis=0, concat_axis=0, tiled=True)

    def to_slots(received):
        spread = received.reshape(bands, slots * 4, levels, lat_rows)
        return jnp.transpose(spread, (1, 2, 0, 3)).reshape(slots, 4 * levels, lat_count)

    def to_bands(piece):
        spread = piece.reshape(slots * 4, levels, bands, lat_rows)
        return jnp.transpose(spread, (2, 0, 1, 3)).reshape(bands, slots * 4, points)

    received_1, sent_0, legendre = lax.optimization_barrier(
        (exchange(to_fourier(1)), to_fourier(0), legendre)
    )
    received_0 = exchange(sent_0)

    rounded = slot_call(
        ("analyse",), truncation, local_waves, to_slots(received_1), legendre, 2 * levels, columns,
    )
    rounded, received_0 = lax.optimization_barrier((rounded, received_0))
    share = -(-slots // layers)
    spare = share * layers - slots
    sent = jnp.pad(rounded, ((0, spare), (0, 0), (0, 0)))
    main, last = sent[:, :, : columns - 1], sent[:, :, columns - 1]

    def gather_levels(block):
        tail = block.shape[2:]
        got = swap(block, "lev")
        got = got.reshape((layers, share, 2, levels) + tail)
        got = jnp.moveaxis(got, 0, 2)
        return got.reshape((share, 2, layers * levels) + tail)

    def scatter_levels(block):
        tail = block.shape[3:]
        put = block.reshape((share, 2, layers, levels) + tail)
        put = jnp.moveaxis(put, 2, 0).reshape((layers * share, 2 * levels) + tail)
        return swap(put, "lev")

    solve_waves = lax.dynamic_slice_in_dim(
        jnp.pad(local_waves, (0, spare)), lax.axis_index("lev") * share, share
    )

    def solve(values, column):
        _, ratio = ratio_of(solve_waves[:, None], column[None, :], truncation)
        projected = jnp.einsum("km,sckj->scmj", modes, values, preferred_element_type=jnp.float32)
        factor = 1.0 / (1.0 + rates[None, :, None] * ratio[:, None, :])
        weighted = (projected * factor[:, None]).astype(jnp.bfloat16)
        return jnp.einsum(
            "vm,scmj->scvj", modes, weighted, preferred_element_type=jnp.float32
        ).astype(jnp.bfloat16)

    column = jnp.arange(columns, dtype=jnp.int32)
    main, last, slots_0 = lax.optimization_barrier(
        (gather_levels(main), gather_levels(last), to_slots(received_0))
    )
    whole = jnp.concatenate([main, last[..., None]], axis=-1)
    solved = solve(whole, column)
    back_main = scatter_levels(solved[..., : columns - 1])
    back_last = scatter_levels(solved[..., columns - 1])

    rows_0 = slot_call(
        ("analyse", "damp", "synthesise"), truncation, local_waves,
        slots_0, legendre, 4 * levels, lat_count,
    )
    back_main, back_last, rows_0 = lax.optimization_barrier((back_main, back_last, rows_0))
    pieces_0 = to_bands(rows_0)
    updated = jnp.concatenate([back_main, back_last[..., None]], axis=-1)[:slots]
    pieces_1 = to_bands(
        slot_call(
            ("synthesise",), truncation, local_waves, updated, legendre, 4 * levels, lat_count
        )
    )
    returned_0, pieces_1 = lax.optimization_barrier((exchange(pieces_0), pieces_1))
    returned_1 = exchange(pieces_1)
    inverse = (expand(parts, imaginary, length) * weight[:, None]).astype(jnp.bfloat16)

    def to_grid(returned):
        return lax.dot_general(
            returned.reshape(-1, points), inverse, (((0,), (0,)), ((), ())), preferred_element_type=jnp.float32
        ).reshape(levels, lat_rows, length)

    return jnp.stack([to_grid(returned_0), to_grid(returned_1)])


def solution(mesh):
    placed = (
        P(None, "lev", "lat", None),
        P(None, "lev", "lat", None),
        P(),
        P("lat", None, None),
        P(),
        P(),
    )
    return jax.shard_map(
        per_device,
        mesh=mesh,
        in_specs=placed,
        out_specs=P(None, "lev", "lat", None),
        check_vma=False,
    )
```

```python
import functools
import math

import jax
import jax.numpy as jnp
from jax import lax
from jax.experimental import pallas as pl
from jax.experimental.pallas import tpu as pltpu
from jax.sharding import PartitionSpec as P


def circle(waves, length):
    step = math.gcd(length, 32)
    coarse = jnp.arange(length // step, dtype=jnp.int32) * step
    fine = jnp.arange(step, dtype=jnp.int32)

    def angles(position):
        turns = (waves[:, None] * position[None, :]) % length
        phases = 2.0 * math.pi / length * turns.astype(jnp.float32)
        return jnp.cos(phases), jnp.sin(phases)

    cos_a, sin_a = angles(coarse)
    cos_b, sin_b = angles(fine)
    return lax.optimization_barrier((cos_a, sin_a, cos_b, sin_b))


def expand(parts, imaginary, length):
    cos_a, sin_a, cos_b, sin_b = parts
    count = cos_a.shape[0]
    wide = lambda t: jnp.repeat(t, length // t.shape[1], axis=1)
    tall = lambda t: jnp.tile(t, (1, length // t.shape[1]))
    ca, sa, cb, sb = wide(cos_a), wide(sin_a), tall(cos_b), tall(sin_b)
    return jnp.where(imaginary[:, None], -(sa * cb + ca * sb), ca * cb - sa * sb)


def ratio_of(wave_a, column, truncation):
    lower = column < truncation - wave_a
    degree = jnp.where(lower, wave_a + column, column - 1)
    ratio = (degree * (degree + 1)).astype(jnp.float32) / float(truncation * (truncation + 1))
    return lower, ratio


def analysed(x, leg, wave_a, truncation, damp):
    rows = x.shape[0] // 2
    product = lax.dot_general(
        x, leg, (((1,), (1,)), ((), ())), preferred_element_type=jnp.float32
    )
    column = lax.broadcasted_iota(jnp.int32, (rows, product.shape[1]), 1)
    lower, ratio = ratio_of(wave_a, column, truncation)
    chosen = jnp.where(lower, product[:rows], product[rows:])
    if damp:
        chosen = chosen / (1.0 + 4.0 * ratio * ratio)
    return chosen.astype(jnp.bfloat16)


def synthesised(values, leg, wave_a, truncation):
    column = lax.broadcasted_iota(jnp.int32, values.shape, 1)
    lower = column < truncation - wave_a
    zero = jnp.zeros_like(values)
    halves = jnp.concatenate([jnp.where(lower, values, zero), jnp.where(lower, zero, values)], axis=0)
    return jnp.dot(halves, leg, preferred_element_type=jnp.float32).astype(jnp.bfloat16)


def slot_kernel(stages, truncation, waves_ref, in_ref, leg_ref, out_ref):
    group = leg_ref.shape[0]
    for i in range(group):
        wave_a = waves_ref[pl.program_id(0) * group + i]
        value, leg = in_ref[i], leg_ref[i]
        if "analyse" in stages:
            value = analysed(value, leg, wave_a, truncation, "damp" in stages)
        if "synthesise" in stages:
            value = synthesised(value, leg, wave_a, truncation)
        out_ref[i] = value


def slot_call(stages, truncation, waves, values, legendre, rows, width):
    slots, columns, lat_count = legendre.shape
    inner = values.shape[1:]
    group = max(g for g in (1, 2, 4) if slots % g == 0)
    return pl.pallas_call(
        functools.partial(slot_kernel, stages, truncation),
        grid_spec=pltpu.PrefetchScalarGridSpec(
            num_scalar_prefetch=1,
            grid=(slots // group,),
            in_specs=[
                pl.BlockSpec((group,) + inner, lambda s, w: (s, 0, 0)),
                pl.BlockSpec((group, columns, lat_count), lambda s, w: (s, 0, 0)),
            ],
            out_specs=pl.BlockSpec((group, rows, width), lambda s, w: (s, 0, 0)),
        ),
        out_shape=jax.ShapeDtypeStruct((slots, rows, width), jnp.bfloat16),
        cost_estimate=pl.CostEstimate(
            flops=2 * slots * max(rows, inner[0]) * lat_count * columns,
            bytes_accessed=2 * slots * (lat_count * columns + inner[0] * inner[1] + rows * width),
            transcendentals=0,
        ),
    )(waves, values, legendre)


def swap(x, axis):
    n = lax.axis_size(axis)
    me = lax.axis_index(axis)
    size = x.shape[0] // n
    pieces = []
    for k in range(n):
        piece = lax.dynamic_slice_in_dim(x, (me + k) % n * size, size, 0)
        if k:
            piece = lax.ppermute(piece, axis, [(i, (i + k) % n) for i in range(n)])
        pieces.append(piece)
    out = jnp.zeros_like(x)
    for k, piece in enumerate(pieces):
        out = lax.dynamic_update_slice_in_dim(out, piece, (me - k + n) % n * size, 0)
    return out


def per_device(grid_adjoint, trajectory, pair_order, legendre, modes, rates):
    fields, levels, lat_rows, length = grid_adjoint.shape
    truncation = length // 2
    slots, lat_count, columns = legendre.shape
    legendre = jnp.transpose(legendre, (0, 2, 1))
    bands = lax.axis_size("lat")
    layers = lax.axis_size("lev")
    points = levels * lat_rows
    pair_order = pair_order.astype(jnp.int32)

    both = jnp.stack([pair_order, truncation - 1 - pair_order], axis=1)
    waves = jnp.repeat(both.reshape(-1), 2)
    imaginary = jnp.arange(4 * pair_order.shape[0]) % 2 == 1
    parts = circle(waves, length)
    forward = (expand(parts, imaginary, length) / length).astype(jnp.bfloat16)
    weight = jnp.where(waves == 0, 1.0, 2.0).astype(jnp.float32)

    local_waves = lax.dynamic_slice_in_dim(pair_order, lax.axis_index("lat") * slots, slots)

    def to_fourier(f):
        own = trajectory[0].astype(jnp.float32) * grid_adjoint[f]
        other = trajectory[1].astype(jnp.float32) * grid_adjoint[1 - f]
        coupled = (own + other).astype(jnp.bfloat16).reshape(points, length)
        fourier = lax.dot_general(
            forward, coupled, (((1,), (1,)), ((), ())), preferred_element_type=jnp.float32
        ).astype(jnp.bfloat16)
        return fourier.reshape(bands, slots * 4, points)

    def exchange(sent):
        return lax.all_to_all(sent, "lat", split_axis=0, concat_axis=0, tiled=True)

    def to_slots(received):
        spread = received.reshape(bands, slots * 4, levels, lat_rows)
        return jnp.transpose(spread, (1, 2, 0, 3)).reshape(slots, 4 * levels, lat_count)

    def to_bands(piece):
        spread = piece.reshape(slots * 4, levels, bands, lat_rows)
        return jnp.transpose(spread, (2, 0, 1, 3)).reshape(bands, slots * 4, points)

    received_1, sent_0, legendre = lax.optimization_barrier(
        (exchange(to_fourier(1)), to_fourier(0), legendre)
    )
    received_0 = exchange(sent_0)

    rounded = slot_call(
        ("analyse",), truncation, local_waves, to_slots(received_1), legendre, 2 * levels, columns,
    )
    rounded, received_0 = lax.optimization_barrier((rounded, received_0))
    share = -(-slots // layers)
    spare = share * layers - slots
    sent = jnp.pad(rounded, ((0, spare), (0, 0), (0, 0)))
    main, last = sent[:, :, : columns - 1], sent[:, :, columns - 1]

    def gather_levels(block):
        tail = block.shape[2:]
        got = swap(block, "lev")
        got = got.reshape((layers, share, 2, levels) + tail)
        got = jnp.moveaxis(got, 0, 2)
        return got.reshape((share, 2, layers * levels) + tail)

    def scatter_levels(block):
        tail = block.shape[3:]
        put = block.reshape((share, 2, layers, levels) + tail)
        put = jnp.moveaxis(put, 2, 0).reshape((layers * share, 2 * levels) + tail)
        return swap(put, "lev")

    solve_waves = lax.dynamic_slice_in_dim(
        jnp.pad(local_waves, (0, spare)), lax.axis_index("lev") * share, share
    )

    def solve(values, column):
        _, ratio = ratio_of(solve_waves[:, None], column[None, :], truncation)
        projected = jnp.einsum("km,sckj->scmj", modes, values, preferred_element_type=jnp.float32)
        factor = 1.0 / (1.0 + rates[None, :, None] * ratio[:, None, :])
        weighted = (projected * factor[:, None]).astype(jnp.bfloat16)
        return jnp.einsum(
            "vm,scmj->scvj", modes, weighted, preferred_element_type=jnp.float32
        ).astype(jnp.bfloat16)

    column = jnp.arange(columns, dtype=jnp.int32)
    main, last, slots_0 = lax.optimization_barrier(
        (gather_levels(main), gather_levels(last), to_slots(received_0))
    )
    whole = jnp.concatenate([main, last[..., None]], axis=-1)
    solved = solve(whole, column)
    back_main = scatter_levels(solved[..., : columns - 1])
    back_last = scatter_levels(solved[..., columns - 1])

    rows_0 = slot_call(
        ("analyse", "damp", "synthesise"), truncation, local_waves,
        slots_0, legendre, 4 * levels, lat_count,
    )
    back_main, back_last, pieces_0 = lax.optimization_barrier(
        (back_main, back_last, to_bands(rows_0))
    )
    updated = jnp.concatenate([back_main, back_last[..., None]], axis=-1)[:slots]
    pieces_1 = to_bands(
        slot_call(
            ("synthesise",), truncation, local_waves, updated, legendre, 4 * levels, lat_count
        )
    )
    returned_0, pieces_1 = lax.optimization_barrier((exchange(pieces_0), pieces_1))
    returned_1 = exchange(pieces_1)
    inverse = (expand(parts, imaginary, length) * weight[:, None]).astype(jnp.bfloat16)

    def to_grid(returned):
        return lax.dot_general(
            returned.reshape(-1, points), inverse, (((0,), (0,)), ((), ())), preferred_element_type=jnp.float32
        ).reshape(levels, lat_rows, length)

    return jnp.stack([to_grid(returned_0), to_grid(returned_1)])


def solution(mesh):
    placed = (
        P(None, "lev", "lat", None),
        P(None, "lev", "lat", None),
        P(),
        P("lat", None, None),
        P(),
        P(),
    )
    return jax.shard_map(
        per_device,
        mesh=mesh,
        in_specs=placed,
        out_specs=P(None, "lev", "lat", None),
        check_vma=False,
    )
```
